32 devices in a mesh: gx: 8 (over y, x, core), gy: 4 (over z).
Axes of the slice: x: 2, y: 2, z: 4, core: 2. Of those that a mesh axis runs over, the one named last changes fastest.
Arguments:
- blocks: bfloat16 [8, 4, 128, 128, 128], P('gx', 'gy'), may hold values from -0.1875 to 0.1875
- pattern: int32 [8, 4, 128], P('gx', 'gy'), may hold values from 0 to 255, as said below
- local_src: bfloat16 [8, 4, 2, 32, 2048], P('gx', 'gy'), may hold values from -4 to 4
- owner: int32 [2, 32], replicated, may hold values from 0 to 31
Outputs:
- sweep_out: bfloat16 [8, 4, 2, 32, 2048], P('gx', 'gy')
The draws below stay inside these ranges and needn't reach their ends.
Inputs may be any that keep to these rules, and one draw needn't show every extreme that they name: `pattern`: the 128 values of one cell are distinct.
All inputs are finite; a program needn't handle non-finite values.
Results may differ from the reference program's by a relative error of at most 0.019.
Values may be sent and summed in bfloat16 or wider, within the bound.
A program may use at most 64 MiB of HBM per device.

```python
import jax
import jax.numpy as jnp
from jax import lax

TR = 1024
BS = 128
NBLK = 16
NNZ = 128
S = 32
NB = 2
NX = 8
NY = 4


def draw_pattern(key, part):
    keys = jax.random.split(key, NX * NY)
    perms = jax.vmap(lambda one_key: jax.random.permutation(one_key, NBLK * NBLK))(keys)
    return perms[:, :NNZ].reshape(NX, NY, NNZ).astype(jnp.int32)


def set_ends(values, stream_key, smallest, high):
    longest = values.shape.index(max(values.shape))
    spots = []
    for shift in (0, 1):
        where = [jax.random.randint(jax.random.fold_in(stream_key, axis), (), 0, length) for axis, length in enumerate(values.shape)]
        where[longest] = (where[longest] + shift) % values.shape[longest]
        spots.append(tuple(where))
    return values.at[spots[0]].set(smallest).at[spots[1]].set(high)


def block_scale(own_key, dims, cuts, low, high):
    factor_of = 1.0
    for dim, parts in cuts:
        steps = jax.random.uniform(jax.random.fold_in(jax.random.fold_in(own_key, 6), dim), (parts,), jnp.float32, low / len(cuts), high / len(cuts))
        factor_of = factor_of * jnp.repeat(jnp.exp(steps), dims[dim] // parts).reshape((-1,) + (1,) * (len(dims) - 1 - dim))
    return factor_of


def centred(rng, dims, spread, limit, pieces=(), kind=jnp.bfloat16):
    gain = block_scale(rng, dims, pieces, -0.22, 0.18) if pieces else 1.0
    drawn = jax.random.normal(rng, dims, jnp.float32) * spread * gain
    return jnp.minimum(jnp.maximum(drawn, -limit), limit).astype(kind)


def setup_inputs(seed: int = 0) -> dict:
    key_of = jax.random.split(jax.random.key(seed), 5)
    return {
        "blocks": centred(key_of[0], (NX, NY, NNZ, BS, BS), (NNZ * BS * BS // (2 * TR)) ** -0.5, 0.1875, ((0, 8), (1, 4))),
        "pattern": draw_pattern(jax.random.fold_in(key_of[4], 71), 0),
        "local_src": centred(key_of[2], (NX, NY, NB, S, 2 * TR), 0.5, 4.0, ((0, 8), (1, 4))),
        "owner": set_ends(jax.random.randint(key_of[3], (NB, S), 0, NX * NY), jax.random.fold_in(key_of[3], 1), 0, (NX * NY) - 1).astype(jnp.int32),
    }


def cell_matrix(blk, pat):
    dense = jnp.zeros((NBLK * NBLK, BS, BS), blk.dtype).at[pat].set(blk)
    return dense.reshape(NBLK, NBLK, BS, BS).transpose(0, 2, 1, 3).reshape(2 * TR, 2 * TR)


def reference(blocks, pattern, local_src, owner):
    cell_ids = jnp.arange(NX * NY, dtype=jnp.int32).reshape(NX, NY)

    def column(left_all, column_data):
        blk_col, pat_col, src_col, id_col = column_data

        def cell(bottom, cell_data):
            left, blk, pat, src, cell_id = cell_data
            joined = jnp.concatenate([left, bottom], axis=2).reshape(NB * S, 2 * TR)
            matrix = cell_matrix(blk, pat)
            total = jnp.dot(joined, matrix.T, preferred_element_type=jnp.float32).reshape(NB, S, 2 * TR)
            mask = (owner == cell_id).astype(jnp.float32)
            total = total + src.astype(jnp.float32) * mask[:, :, None]
            result = total.astype(jnp.bfloat16)
            return result[:, :, TR:], result

        zero = jnp.zeros((NB, S, TR), jnp.bfloat16)
        _, results = lax.scan(cell, zero, (left_all, blk_col, pat_col, src_col, id_col))
        return results[:, :, :, :TR], results

    start = jnp.zeros((NY, NB, S, TR), jnp.bfloat16)
    _, outputs = lax.scan(column, start, (blocks, pattern, local_src, cell_ids))
    return outputs
```

```python
import functools

import jax
import jax.numpy as jnp
from jax import lax
from jax.experimental import pallas as pl
from jax.experimental.pallas import tpu as pltpu
from jax.sharding import PartitionSpec as P

MESH = pl.DeviceIdType.MESH
GROUPS = 2
CHUNK = 256
PARTS = 4


def kernel(
    dims,
    blocks_hbm,
    pattern_hbm,
    src_hbm,
    owner_hbm,
    out_ref,
    blk,
    pat_v,
    own_v,
    src_v,
    inv_v,
    inv_s,
    acc,
    inbuf,
    outbuf,
    load_sem,
    send_sem,
    recv_sem,
):
    nx, ny, nnz, order, rows, width = dims
    trace = width // 2
    nblk = width // order
    group = rows // GROUPS
    per_dir = trace // CHUNK
    sub = CHUNK // order
    me_x = lax.axis_index("gx")
    me_y = lax.axis_index("gy")
    has = (me_x > 0, me_y > 0)
    sends = (me_x < nx - 1, me_y < ny - 1)
    before = ((me_x - 1, me_y), (me_x, me_y - 1))
    after = ((me_x + 1, me_y), (me_x, me_y + 1))

    barrier = pltpu.get_barrier_semaphore()
    for d in range(2):

        @pl.when(has[d])
        def _():
            pl.semaphore_signal(barrier, inc=1, device_id=before[d], device_id_type=MESH)

    pat_copy = pltpu.make_async_copy(pattern_hbm, pat_v, load_sem.at[0])
    own_copy = pltpu.make_async_copy(owner_hbm, own_v, load_sem.at[1])
    src_copy = pltpu.make_async_copy(src_hbm, src_v, load_sem.at[2])
    pat_copy.start()
    own_copy.start()
    src_copy.start()
    step = nnz // PARTS
    blk_copies = [
        pltpu.make_async_copy(
            blocks_hbm.at[pl.ds(p * step, step)],
            blk.at[pl.ds(p * step, step)],
            load_sem.at[3 + p],
        )
        for p in range(PARTS)
    ]
    for copy in blk_copies:
        copy.start()
    blk[nnz] = jnp.zeros((order, order), blk.dtype)

    own_copy.wait()
    src_copy.wait()
    cell_id = me_x * ny + me_y
    nbatch, nsource = own_v.shape
    eye = lax.broadcasted_iota(jnp.int32, (nsource, nsource), 0) == lax.broadcasted_iota(
        jnp.int32, (nsource, nsource), 1
    )
    for b in range(nbatch):
        mine = (own_v[b : b + 1, :] == cell_id).astype(jnp.float32)
        mask = jnp.sum(jnp.where(eye, mine, 0.0), axis=1, keepdims=True)
        span = pl.ds(b * nsource, nsource)
        acc[span, :] = src_v[span, :].astype(jnp.float32) * mask

    pat_copy.wait()
    pat_t = jnp.transpose(jnp.broadcast_to(pat_v[...], (nnz, nnz)))
    lane = lax.broadcasted_iota(jnp.int32, (nnz, nnz), 1)
    which = lax.broadcasted_iota(jnp.int32, (nnz, nnz), 0)
    for h in range(nblk * nblk // nnz):
        hit = jnp.where(pat_t == lane + h * nnz, which, nnz)
        inv_v[h : h + 1, :] = jnp.min(hit, axis=0, keepdims=True)
    inv_copy = pltpu.make_async_copy(inv_v, inv_s, load_sem.at[3 + PARTS])
    inv_copy.start()
    inv_copy.wait()

    wanted = sum(s.astype(jnp.int32) for s in sends)

    @pl.when(wanted > 0)
    def _():
        pl.semaphore_wait(barrier, wanted)

    def transfer(g, d, c):
        return pltpu.make_async_remote_copy(
            src_ref=outbuf.at[g, d, c],
            dst_ref=inbuf.at[g, d, c],
            send_sem=send_sem.at[g, d, c],
            recv_sem=recv_sem.at[g, d, c],
            device_id=after[d],
            device_id_type=MESH,
        )

    def weights(o, k):
        rows_of = []
        for a in range(sub):
            parts = []
            for b in range(sub):
                f = (o * sub + a) * nblk + k * sub + b
                parts.append(blk[inv_s[f // nnz, f % nnz]])
            rows_of.append(jnp.concatenate(parts, axis=1))
        return jnp.concatenate(rows_of, axis=0)

    def product(g, d, c, o):
        return lax.dot_general(
            inbuf[g, d, c],
            weights(o, d * per_dir + c),
            (((1,), (1,)), ((), ())),
            preferred_element_type=jnp.float32,
        )

    def emit(g, d, c, value):
        o = d * per_dir + c
        result = value.astype(jnp.bfloat16)
        outbuf[g, d, c] = result
        out_ref[pl.ds(g * group, group), pl.ds(o * CHUNK, CHUNK)] = result

        @pl.when(sends[d])
        def _():
            transfer(g, d, c).start()

    order_out = [(d, c) for c in range(per_dir) for d in range(2)]
    for copy in blk_copies:
        copy.wait()
    for g in range(GROUPS):
        span = pl.ds(g * group, group)
        for c in range(per_dir):
            for d in range(2):
                last = d == 1 and c == per_dir - 1

                @pl.when(has[d])
                def _():
                    transfer(g, d, c).wait_recv()
                    for od, oc in order_out:
                        o = od * per_dir + oc
                        at = (span, pl.ds(o * CHUNK, CHUNK))
                        value = acc[at] + product(g, d, c, o)
                        if last:
                            emit(g, od, oc, value)
                        else:
                            acc[at] = value

                if last:

                    @pl.when(jnp.logical_not(has[d]))
                    def _():
                        for od, oc in order_out:
                            o = od * per_dir + oc
                            emit(g, od, oc, acc[span, pl.ds(o * CHUNK, CHUNK)])

    for g in range(GROUPS):
        for d, c in order_out:

            @pl.when(sends[d])
            def _():
                transfer(g, d, c).wait_send()


def body(nx, ny, blocks, pattern, local_src, owner):
    nnz, order = blocks.shape[2], blocks.shape[3]
    nbatch, nsource, width = local_src.shape[2:]
    rows = nbatch * nsource
    nblk = width // order
    per_dir = width // 2 // CHUNK
    group = rows // GROUPS
    dims = (nx, ny, nnz, order, rows, width)
    any_spec = pl.BlockSpec(memory_space=pl.ANY)
    result = pl.pallas_call(
        functools.partial(kernel, dims),
        name="sweep",
        out_shape=jax.ShapeDtypeStruct((rows, width), jnp.bfloat16),
        in_specs=[any_spec] * 4,
        out_specs=pl.BlockSpec(memory_space=pltpu.VMEM),
        scratch_shapes=[
            pltpu.VMEM((nnz + 1, order, order), jnp.bfloat16),
            pltpu.VMEM((1, nnz), jnp.int32),
            pltpu.VMEM((nbatch, nsource), jnp.int32),
            pltpu.VMEM((rows, width), jnp.bfloat16),
            pltpu.VMEM((nblk * nblk // nnz, nnz), jnp.int32),
            pltpu.SMEM((nblk * nblk // nnz, nnz), jnp.int32),
            pltpu.VMEM((rows, width), jnp.float32),
            pltpu.VMEM((GROUPS, 2, per_dir, group, CHUNK), jnp.bfloat16),
            pltpu.VMEM((GROUPS, 2, per_dir, group, CHUNK), jnp.bfloat16),
            pltpu.SemaphoreType.DMA((4 + PARTS,)),
            pltpu.SemaphoreType.DMA((GROUPS, 2, per_dir)),
            pltpu.SemaphoreType.DMA((GROUPS, 2, per_dir)),
        ],
        compiler_params=pltpu.CompilerParams(collective_id=0, has_side_effects=True),
    )(
        blocks.reshape(nnz, order, order),
        pattern.reshape(1, nnz),
        local_src.reshape(rows, width),
        owner,
    )
    return result.reshape(1, 1, nbatch, nsource, width)


def solution(mesh):
    return jax.shard_map(
        functools.partial(body, mesh.shape["gx"], mesh.shape["gy"]),
        mesh=mesh,
        in_specs=(
            P("gx", "gy", None, None, None),
            P("gx", "gy", None),
            P("gx", "gy", None, None, None),
            P(),
        ),
        out_specs=P("gx", "gy", None, None, None),
        check_vma=False,
    )
```

```python
import functools

import jax
import jax.numpy as jnp
from jax import lax
from jax.experimental import pallas as pl
from jax.experimental.pallas import tpu as pltpu
from jax.sharding import PartitionSpec as P

MESH = pl.DeviceIdType.MESH
GROUPS = 2
CHUNK = 256
PARTS = 4
UNROLL = 8


def kernel(
    dims,
    blocks_hbm,
    pattern_hbm,
    src_hbm,
    owner_hbm,
    out_ref,
    blk,
    pat_v,
    own_v,
    src_v,
    inv_v,
    inv_s,
    acc,
    inbuf,
    outbuf,
    load_sem,
    send_sem,
    recv_sem,
):
    nx, ny, nnz, order, rows, width = dims
    trace = width // 2
    nblk = width // order
    group = rows // GROUPS
    per_dir = trace // CHUNK
    sub = CHUNK // order
    me_x = lax.axis_index("gx")
    me_y = lax.axis_index("gy")
    has = (me_x > 0, me_y > 0)
    sends = (me_x < nx - 1, me_y < ny - 1)
    before = ((me_x - 1, me_y), (me_x, me_y - 1))
    after = ((me_x + 1, me_y), (me_x, me_y + 1))

    barrier = pltpu.get_barrier_semaphore()
    for d in range(2):

        @pl.when(has[d])
        def _():
            pl.semaphore_signal(barrier, inc=1, device_id=before[d], device_id_type=MESH)

    pat_copy = pltpu.make_async_copy(pattern_hbm, pat_v, load_sem.at[0])
    own_copy = pltpu.make_async_copy(owner_hbm, own_v, load_sem.at[1])
    src_copy = pltpu.make_async_copy(src_hbm, src_v, load_sem.at[2])
    pat_copy.start()
    own_copy.start()
    src_copy.start()
    step = nnz // PARTS
    blk_copies = [
        pltpu.make_async_copy(
            blocks_hbm.at[pl.ds(p * step, step)],
            blk.at[pl.ds(p * step, step)],
            load_sem.at[3 + p],
        )
        for p in range(PARTS)
    ]
    for copy in blk_copies:
        copy.start()
    blk[nnz] = jnp.zeros((order, order), blk.dtype)

    own_copy.wait()
    src_copy.wait()
    cell_id = me_x * ny + me_y
    nbatch, nsource = own_v.shape
    eye = lax.broadcasted_iota(jnp.int32, (nsource, nsource), 0) == lax.broadcasted_iota(
        jnp.int32, (nsource, nsource), 1
    )
    for b in range(nbatch):
        mine = (own_v[b : b + 1, :] == cell_id).astype(jnp.float32)
        mask = jnp.sum(jnp.where(eye, mine, 0.0), axis=1, keepdims=True)
        span = pl.ds(b * nsource, nsource)
        acc[span, :] = src_v[span, :].astype(jnp.float32) * mask

    wanted = sum(s.astype(jnp.int32) for s in sends)

    @pl.when(wanted > 0)
    def _():
        pl.semaphore_wait(barrier, wanted)

    def transfer(g, d, c):
        return pltpu.make_async_remote_copy(
            src_ref=outbuf.at[g, d, c],
            dst_ref=inbuf.at[g, d, c],
            send_sem=send_sem.at[g, d, c],
            recv_sem=recv_sem.at[g, d, c],
            device_id=after[d],
            device_id_type=MESH,
        )

    def weights(o, k):
        rows_of = []
        for b in range(sub):
            parts = []
            for a in range(sub):
                f = (o * sub + a) * nblk + k * sub + b
                parts.append(blk[inv_s[f // nnz, f % nnz]])
            rows_of.append(jnp.concatenate(parts, axis=1))
        return jnp.concatenate(rows_of, axis=0)

    def product(g, d, c, o):
        return jnp.dot(
            inbuf[g, d, c],
            weights(o, d * per_dir + c),
            preferred_element_type=jnp.float32,
        )

    def emit(g, d, c, value):
        o = d * per_dir + c
        result = value.astype(jnp.bfloat16)
        outbuf[g, d, c] = result
        out_ref[pl.ds(g * group, group), pl.ds(o * CHUNK, CHUNK)] = result

        @pl.when(sends[d])
        def _():
            transfer(g, d, c).start()

    def place(g, d, c):
        return (pl.ds(g * group, group), pl.ds((d * per_dir + c) * CHUNK, CHUNK))

    ordered = [(d, c) for c in range(per_dir) for d in range(2)]
    head, tail = ordered[:per_dir], ordered[per_dir:]
    any_input = jnp.logical_or(has[0], has[1])

    @pl.when(jnp.logical_not(any_input))
    def _():
        for g in range(GROUPS):
            for d, c in ordered:
                emit(g, d, c, acc[place(g, d, c)])
        pat_copy.wait()
        for copy in blk_copies:
            copy.wait()

    @pl.when(any_input)
    def _():
        for d in range(2):

            @pl.when(jnp.logical_not(has[d]))
            def _():
                for g in range(GROUPS):
                    for td, c in tail:
                        if td == d:
                            inbuf[g, d, c] = jnp.zeros((group, CHUNK), inbuf.dtype)

        pat_copy.wait()
        pat_t = jnp.transpose(jnp.broadcast_to(pat_v[...], (nnz, nnz)))
        lane = lax.broadcasted_iota(jnp.int32, (nnz, nnz), 1)
        which = lax.broadcasted_iota(jnp.int32, (nnz, nnz), 0)
        for h in range(nblk * nblk // nnz):
            hit = jnp.where(pat_t == lane + h * nnz, which, nnz)
            inv_v[h : h + 1, :] = jnp.min(hit, axis=0, keepdims=True)
        inv_copy = pltpu.make_async_copy(inv_v, inv_s, load_sem.at[3 + PARTS])
        inv_copy.start()
        inv_copy.wait()

        for p, copy in enumerate(blk_copies):
            copy.wait()

            def turn(i, carry):
                for u in range(UNROLL):
                    at = p * step + i * UNROLL + u
                    blk[at] = jnp.transpose(blk[at])
                return carry

            lax.fori_loop(0, step // UNROLL, turn, 0)

        for g in range(GROUPS):
            for d, c in head:

                @pl.when(has[d])
                def _():
                    transfer(g, d, c).wait_recv()
                    for od, oc in ordered:
                        at = place(g, od, oc)
                        acc[at] = acc[at] + product(g, d, c, od * per_dir + oc)

            for d in range(2):

                @pl.when(has[d])
                def _():
                    for td, c in tail:
                        if td == d:
                            transfer(g, d, c).wait_recv()

            for od, oc in ordered:
                value = acc[place(g, od, oc)]
                for d, c in tail:
                    value = value + product(g, d, c, od * per_dir + oc)
                emit(g, od, oc, value)

    for g in range(GROUPS):
        for d, c in ordered:

            @pl.when(sends[d])
            def _():
                transfer(g, d, c).wait_send()


def body(nx, ny, blocks, pattern, local_src, owner):
    nnz, order = blocks.shape[2], blocks.shape[3]
    nbatch, nsource, width = local_src.shape[2:]
    rows = nbatch * nsource
    nblk = width // order
    per_dir = width // 2 // CHUNK
    group = rows // GROUPS
    dims = (nx, ny, nnz, order, rows, width)
    any_spec = pl.BlockSpec(memory_space=pl.ANY)
    result = pl.pallas_call(
        functools.partial(kernel, dims),
        name="sweep",
        out_shape=pltpu.VMEM((rows, width), jnp.bfloat16),
        in_specs=[any_spec] * 4,
        out_specs=pl.BlockSpec(memory_space=pltpu.VMEM),
        scratch_shapes=[
            pltpu.VMEM((nnz + 1, order, order), jnp.bfloat16),
            pltpu.VMEM((1, nnz), jnp.int32),
            pltpu.VMEM((nbatch, nsource), jnp.int32),
            pltpu.VMEM((rows, width), jnp.bfloat16),
            pltpu.VMEM((nblk * nblk // nnz, nnz), jnp.int32),
            pltpu.SMEM((nblk * nblk // nnz, nnz), jnp.int32),
            pltpu.VMEM((rows, width), jnp.float32),
            pltpu.VMEM((GROUPS, 2, per_dir, group, CHUNK), jnp.bfloat16),
            pltpu.VMEM((GROUPS, 2, per_dir, group, CHUNK), jnp.bfloat16),
            pltpu.SemaphoreType.DMA((4 + PARTS,)),
            pltpu.SemaphoreType.DMA((GROUPS, 2, per_dir)),
            pltpu.SemaphoreType.DMA((GROUPS, 2, per_dir)),
        ],
        compiler_params=pltpu.CompilerParams(collective_id=0, has_side_effects=True),
    )(
        blocks.reshape(nnz, order, order),
        pattern.reshape(1, nnz),
        local_src.reshape(rows, width),
        owner,
    )
    return result.reshape(1, 1, nbatch, nsource, width)


def solution(mesh):
    return jax.shard_map(
        functools.partial(body, mesh.shape["gx"], mesh.shape["gy"]),
        mesh=mesh,
        in_specs=(
            P("gx", "gy", None, None, None),
            P("gx", "gy", None),
            P("gx", "gy", None, None, None),
            P(),
        ),
        out_specs=P("gx", "gy", None, None, None),
        check_vma=False,
    )
```

```python
import functools

import jax
import jax.numpy as jnp
from jax import lax
from jax.experimental import pallas as pl
from jax.experimental.pallas import tpu as pltpu
from jax.sharding import PartitionSpec as P

MESH = pl.DeviceIdType.MESH
GROUPS = 2
CHUNK = 256
PARTS = 4
INFLIGHT = 4
HEAD = 2
UNROLL = 16


def kernel(
    dims,
    blocks_hbm,
    pattern_hbm,
    src_hbm,
    owner_hbm,
    out_ref,
    blk,
    pat_v,
    own_v,
    src_v,
    inv_v,
    inv_s,
    acc,
    inbuf,
    outbuf,
    load_sem,
    send_sem,
    recv_sem,
):
    nx, ny, nnz, order, rows, width = dims
    trace = width // 2
    nblk = width // order
    group = rows // GROUPS
    per_dir = trace // CHUNK
    sub = CHUNK // order
    me_x = lax.axis_index("gx")
    me_y = lax.axis_index("gy")
    has = (me_x > 0, me_y > 0)
    sends = (me_x < nx - 1, me_y < ny - 1)
    before = ((me_x - 1, me_y), (me_x, me_y - 1))
    after = ((me_x + 1, me_y), (me_x, me_y + 1))

    barrier = pltpu.get_barrier_semaphore()
    for d in range(2):

        @pl.when(has[d])
        def _():
            pl.semaphore_signal(barrier, inc=1, device_id=before[d], device_id_type=MESH)

    pat_copy = pltpu.make_async_copy(pattern_hbm, pat_v, load_sem.at[0])
    own_copy = pltpu.make_async_copy(owner_hbm, own_v, load_sem.at[1])
    src_copy = pltpu.make_async_copy(src_hbm, src_v, load_sem.at[2])
    pat_copy.start()
    own_copy.start()
    src_copy.start()
    step = nnz // PARTS
    blk_copies = [
        pltpu.make_async_copy(
            blocks_hbm.at[pl.ds(p * step, step)],
            blk.at[pl.ds(p * step, step)],
            load_sem.at[3 + p],
        )
        for p in range(PARTS)
    ]
    for copy in blk_copies[:INFLIGHT]:
        copy.start()
    blk[nnz] = jnp.zeros((order, order), blk.dtype)

    own_copy.wait()
    src_copy.wait()
    cell_id = me_x * ny + me_y
    nbatch, nsource = own_v.shape
    eye = lax.broadcasted_iota(jnp.int32, (nsource, nsource), 0) == lax.broadcasted_iota(
        jnp.int32, (nsource, nsource), 1
    )
    for b in range(nbatch):
        mine = (own_v[b : b + 1, :] == cell_id).astype(jnp.float32)
        mask = jnp.sum(jnp.where(eye, mine, 0.0), axis=1, keepdims=True)
        span = pl.ds(b * nsource, nsource)
        acc[span, :] = src_v[span, :].astype(jnp.float32) * mask

    wanted = sum(s.astype(jnp.int32) for s in sends)

    @pl.when(wanted > 0)
    def _():
        pl.semaphore_wait(barrier, wanted)

    def transfer(g, d, c):
        return pltpu.make_async_remote_copy(
            src_ref=outbuf.at[g, d, c],
            dst_ref=inbuf.at[g, d, c],
            send_sem=send_sem.at[g, d, c],
            recv_sem=recv_sem.at[g, d, c],
            device_id=after[d],
            device_id_type=MESH,
        )

    def weights(o, k):
        rows_of = []
        for b in range(sub):
            parts = []
            for a in range(sub):
                f = (o * sub + a) * nblk + k * sub + b
                parts.append(blk[inv_s[f // nnz, f % nnz]])
            rows_of.append(jnp.concatenate(parts, axis=1))
        return jnp.concatenate(rows_of, axis=0)

    def product(g, d, c, outs):
        wide = [weights(o, d * per_dir + c) for o in outs]
        return jnp.dot(
            inbuf[g, d, c],
            jnp.concatenate(wide, axis=1),
            preferred_element_type=jnp.float32,
        )

    def emit(g, d, c, value):
        o = d * per_dir + c
        result = value.astype(jnp.bfloat16)
        outbuf[g, d, c] = result
        out_ref[pl.ds(g * group, group), pl.ds(o * CHUNK, CHUNK)] = result

        @pl.when(sends[d])
        def _():
            transfer(g, d, c).start()

    def place(g, d, c):
        return (pl.ds(g * group, group), pl.ds((d * per_dir + c) * CHUNK, CHUNK))

    ordered = [(d, c) for c in range(per_dir) for d in range(2)]
    any_input = jnp.logical_or(has[0], has[1])

    @pl.when(jnp.logical_not(any_input))
    def _():
        for g in range(GROUPS):
            for d, c in ordered:
                emit(g, d, c, acc[place(g, d, c)])
        pat_copy.wait()
        for copy in blk_copies[:INFLIGHT]:
            copy.wait()

    @pl.when(any_input)
    def _():
        pat_copy.wait()
        pat_t = jnp.transpose(jnp.broadcast_to(pat_v[...], (nnz, nnz)))
        lane = lax.broadcasted_iota(jnp.int32, (nnz, nnz), 1)
        which = lax.broadcasted_iota(jnp.int32, (nnz, nnz), 0)
        for h in range(nblk * nblk // nnz):
            hit = jnp.where(pat_t == lane + h * nnz, which, nnz)
            inv_v[h : h + 1, :] = jnp.min(hit, axis=0, keepdims=True)
        inv_copy = pltpu.make_async_copy(inv_v, inv_s, load_sem.at[3 + PARTS])
        inv_copy.start()
        inv_copy.wait()

        for p, copy in enumerate(blk_copies):
            copy.wait()
            if p + INFLIGHT < PARTS:
                blk_copies[p + INFLIGHT].start()

            def turn(i, carry):
                for u in range(UNROLL):
                    at = p * step + i * UNROLL + u
                    blk[at] = jnp.transpose(blk[at])
                return carry

            lax.fori_loop(0, step // UNROLL, turn, 0)

        def apply(g, dirs):
            for c in range(HEAD):
                for d in dirs:
                    transfer(g, d, c).wait_recv()
                for oc in range(per_dir):
                    both = sum(product(g, d, c, (oc, per_dir + oc)) for d in dirs)
                    for od in range(2):
                        at = place(g, od, oc)
                        acc[at] = acc[at] + both[:, od * CHUNK : (od + 1) * CHUNK]
            for c in range(HEAD, per_dir):
                for d in dirs:
                    transfer(g, d, c).wait_recv()
            for oc in range(per_dir):
                both = sum(
                    product(g, d, c, (oc, per_dir + oc))
                    for c in range(HEAD, per_dir)
                    for d in dirs
                )
                for od in range(2):
                    value = acc[place(g, od, oc)] + both[:, od * CHUNK : (od + 1) * CHUNK]
                    emit(g, od, oc, value)

        for dirs in ((0, 1), (0,), (1,)):
            here = [has[d] if d in dirs else jnp.logical_not(has[d]) for d in range(2)]

            @pl.when(jnp.logical_and(here[0], here[1]))
            def _():
                for g in range(GROUPS):
                    apply(g, dirs)

    for g in range(GROUPS):
        for d, c in ordered:

            @pl.when(sends[d])
            def _():
                transfer(g, d, c).wait_send()


def body(nx, ny, blocks, pattern, local_src, owner):
    nnz, order = blocks.shape[2], blocks.shape[3]
    nbatch, nsource, width = local_src.shape[2:]
    rows = nbatch * nsource
    nblk = width // order
    per_dir = width // 2 // CHUNK
    group = rows // GROUPS
    dims = (nx, ny, nnz, order, rows, width)
    any_spec = pl.BlockSpec(memory_space=pl.ANY)
    result = pl.pallas_call(
        functools.partial(kernel, dims),
        name="sweep",
        out_shape=pltpu.VMEM((rows, width), jnp.bfloat16),
        in_specs=[any_spec] * 4,
        out_specs=pl.BlockSpec(memory_space=pltpu.VMEM),
        scratch_shapes=[
            pltpu.VMEM((nnz + 1, order, order), jnp.bfloat16),
            pltpu.VMEM((1, nnz), jnp.int32),
            pltpu.VMEM((nbatch, nsource), jnp.int32),
            pltpu.VMEM((rows, width), jnp.bfloat16),
            pltpu.VMEM((nblk * nblk // nnz, nnz), jnp.int32),
            pltpu.SMEM((nblk * nblk // nnz, nnz), jnp.int32),
            pltpu.VMEM((rows, width), jnp.float32),
            pltpu.VMEM((GROUPS, 2, per_dir, group, CHUNK), jnp.bfloat16),
            pltpu.VMEM((GROUPS, 2, per_dir, group, CHUNK), jnp.bfloat16),
            pltpu.SemaphoreType.DMA((4 + PARTS,)),
            pltpu.SemaphoreType.DMA((GROUPS, 2, per_dir)),
            pltpu.SemaphoreType.DMA((GROUPS, 2, per_dir)),
        ],
        compiler_params=pltpu.CompilerParams(collective_id=0, has_side_effects=True),
    )(
        blocks.reshape(nnz, order, order),
        pattern.reshape(1, nnz),
        local_src.reshape(rows, width),
        owner,
    )
    return result.reshape(1, 1, nbatch, nsource, width)


def solution(mesh):
    return jax.shard_map(
        functools.partial(body, mesh.shape["gx"], mesh.shape["gy"]),
        mesh=mesh,
        in_specs=(
            P("gx", "gy", None, None, None),
            P("gx", "gy", None),
            P("gx", "gy", None, None, None),
            P(),
        ),
        out_specs=P("gx", "gy", None, None, None),
        check_vma=False,
    )
```

```python
import functools

import jax
import jax.numpy as jnp
from jax import lax
from jax.experimental import pallas as pl
from jax.experimental.pallas import tpu as pltpu
from jax.sharding import PartitionSpec as P

MESH = pl.DeviceIdType.MESH
GROUPS = 2
CHUNK = 256
PARTS = 4
HEAD = 2
UNROLL = 16


def kernel(
    dims,
    blocks_hbm,
    pattern_hbm,
    src_hbm,
    owner_hbm,
    out_ref,
    blk,
    pat_v,
    own_v,
    src_v,
    inv_v,
    inv_s,
    acc,
    inbuf,
    outbuf,
    load_sem,
    send_sem,
    recv_sem,
):
    nx, ny, nnz, order, rows, width = dims
    trace = width // 2
    nblk = width // order
    group = rows // GROUPS
    per_dir = trace // CHUNK
    sub = CHUNK // order
    me_x = lax.axis_index("gx")
    me_y = lax.axis_index("gy")
    has = (me_x > 0, me_y > 0)
    sends = (me_x < nx - 1, me_y < ny - 1)
    before = ((me_x - 1, me_y), (me_x, me_y - 1))
    after = ((me_x + 1, me_y), (me_x, me_y + 1))

    barrier = pltpu.get_barrier_semaphore()
    for d in range(2):

        @pl.when(has[d])
        def _():
            pl.semaphore_signal(barrier, inc=1, device_id=before[d], device_id_type=MESH)

    pat_copy = pltpu.make_async_copy(pattern_hbm, pat_v, load_sem.at[0])
    own_copy = pltpu.make_async_copy(owner_hbm, own_v, load_sem.at[1])
    src_copy = pltpu.make_async_copy(src_hbm, src_v, load_sem.at[2])
    pat_copy.start()
    own_copy.start()
    src_copy.start()
    step = nnz // PARTS
    blk_copies = [
        pltpu.make_async_copy(
            blocks_hbm.at[pl.ds(p * step, step)],
            blk.at[pl.ds(p * step, step)],
            load_sem.at[3 + p],
        )
        for p in range(PARTS)
    ]
    for copy in blk_copies:
        copy.start()
    blk[nnz] = jnp.zeros((order, order), blk.dtype)

    own_copy.wait()
    src_copy.wait()
    cell_id = me_x * ny + me_y
    nbatch, nsource = own_v.shape
    eye = lax.broadcasted_iota(jnp.int32, (nsource, nsource), 0) == lax.broadcasted_iota(
        jnp.int32, (nsource, nsource), 1
    )
    for b in range(nbatch):
        mine = (own_v[b : b + 1, :] == cell_id).astype(jnp.float32)
        mask = jnp.sum(jnp.where(eye, mine, 0.0), axis=1, keepdims=True)
        span = pl.ds(b * nsource, nsource)
        acc[span, :] = src_v[span, :].astype(jnp.float32) * mask

    wanted = sum(s.astype(jnp.int32) for s in sends)

    @pl.when(wanted > 0)
    def _():
        pl.semaphore_wait(barrier, wanted)

    def transfer(g, d, c):
        return pltpu.make_async_remote_copy(
            src_ref=outbuf.at[g, d, c],
            dst_ref=inbuf.at[g, d, c],
            send_sem=send_sem.at[g, d, c],
            recv_sem=recv_sem.at[g, d, c],
            device_id=after[d],
            device_id_type=MESH,
        )

    def weights(o, k):
        rows_of = []
        for b in range(sub):
            parts = []
            for a in range(sub):
                f = (o * sub + a) * nblk + k * sub + b
                parts.append(blk[inv_s[f // nnz, f % nnz]])
            rows_of.append(jnp.concatenate(parts, axis=1))
        return jnp.concatenate(rows_of, axis=0)

    def as_stored(o, k):
        rows_of = []
        for a in range(sub):
            f = (o * sub + a) * nblk + k * sub
            parts = [blk[inv_s[(f + b) // nnz, (f + b) % nnz]] for b in range(sub)]
            rows_of.append(jnp.concatenate(parts, axis=1))
        return jnp.concatenate(rows_of, axis=0)

    def product(g, d, c, outs, stored):
        if stored:
            tall = [as_stored(o, d * per_dir + c) for o in outs]
            return lax.dot_general(
                inbuf[g, d, c],
                jnp.concatenate(tall, axis=0),
                (((1,), (1,)), ((), ())),
                preferred_element_type=jnp.float32,
            )
        wide = [weights(o, d * per_dir + c) for o in outs]
        return jnp.dot(
            inbuf[g, d, c],
            jnp.concatenate(wide, axis=1),
            preferred_element_type=jnp.float32,
        )

    def emit(g, d, c, value):
        o = d * per_dir + c
        result = value.astype(jnp.bfloat16)
        outbuf[g, d, c] = result
        out_ref[pl.ds(g * group, group), pl.ds(o * CHUNK, CHUNK)] = result

        @pl.when(sends[d])
        def _():
            transfer(g, d, c).start()

    def place(g, d, c):
        return (pl.ds(g * group, group), pl.ds((d * per_dir + c) * CHUNK, CHUNK))

    ordered = [(d, c) for c in range(per_dir) for d in range(2)]
    early = me_x + me_y == 1
    any_input = jnp.logical_or(has[0], has[1])

    @pl.when(jnp.logical_not(any_input))
    def _():
        for g in range(GROUPS):
            for d, c in ordered:
                emit(g, d, c, acc[place(g, d, c)])
        pat_copy.wait()
        for copy in blk_copies:
            copy.wait()

    @pl.when(any_input)
    def _():
        pat_copy.wait()
        pat_t = jnp.transpose(jnp.broadcast_to(pat_v[...], (nnz, nnz)))
        lane = lax.broadcasted_iota(jnp.int32, (nnz, nnz), 1)
        which = lax.broadcasted_iota(jnp.int32, (nnz, nnz), 0)
        for h in range(nblk * nblk // nnz):
            hit = jnp.where(pat_t == lane + h * nnz, which, nnz)
            inv_v[h : h + 1, :] = jnp.min(hit, axis=0, keepdims=True)
        inv_copy = pltpu.make_async_copy(inv_v, inv_s, load_sem.at[3 + PARTS])
        inv_copy.start()
        inv_copy.wait()

        for p, copy in enumerate(blk_copies):
            copy.wait()

            def turn(i, carry):
                for u in range(UNROLL):
                    at = p * step + i * UNROLL + u
                    blk[at] = jnp.transpose(blk[at])
                return carry

            @pl.when(jnp.logical_not(early))
            def _():
                lax.fori_loop(0, step // UNROLL, turn, 0)

        def apply(g, dirs, stored):
            for c in range(HEAD):
                for d in dirs:
                    transfer(g, d, c).wait_recv()
                for oc in range(per_dir):
                    both = sum(product(g, d, c, (oc, per_dir + oc), stored) for d in dirs)
                    for od in range(2):
                        at = place(g, od, oc)
                        acc[at] = acc[at] + both[:, od * CHUNK : (od + 1) * CHUNK]
            for c in range(HEAD, per_dir):
                for d in dirs:
                    transfer(g, d, c).wait_recv()
            for oc in range(per_dir):
                both = sum(
                    product(g, d, c, (oc, per_dir + oc), stored)
                    for c in range(HEAD, per_dir)
                    for d in dirs
                )
                for od in range(2):
                    value = acc[place(g, od, oc)] + both[:, od * CHUNK : (od + 1) * CHUNK]
                    emit(g, od, oc, value)

        for dirs in ((0, 1), (0,), (1,)):
            here = [has[d] if d in dirs else jnp.logical_not(has[d]) for d in range(2)]
            for stored in (False, True) if len(dirs) == 1 else (False,):
                when = early if stored else jnp.logical_not(early)

                @pl.when(jnp.logical_and(jnp.logical_and(here[0], here[1]), when))
                def _():
                    for g in range(GROUPS):
                        apply(g, dirs, stored)

    for g in range(GROUPS):
        for d, c in ordered:

            @pl.when(sends[d])
            def _():
                transfer(g, d, c).wait_send()


def body(nx, ny, blocks, pattern, local_src, owner):
    nnz, order = blocks.shape[2], blocks.shape[3]
    nbatch, nsource, width = local_src.shape[2:]
    rows = nbatch * nsource
    nblk = width // order
    per_dir = width // 2 // CHUNK
    group = rows // GROUPS
    dims = (nx, ny, nnz, order, rows, width)
    any_spec = pl.BlockSpec(memory_space=pl.ANY)
    result = pl.pallas_call(
        functools.partial(kernel, dims),
        name="sweep",
        out_shape=pltpu.VMEM((rows, width), jnp.bfloat16),
        in_specs=[any_spec] * 4,
        out_specs=pl.BlockSpec(memory_space=pltpu.VMEM),
        scratch_shapes=[
            pltpu.VMEM((nnz + 1, order, order), jnp.bfloat16),
            pltpu.VMEM((1, nnz), jnp.int32),
            pltpu.VMEM((nbatch, nsource), jnp.int32),
            pltpu.VMEM((rows, width), jnp.bfloat16),
            pltpu.VMEM((nblk * nblk // nnz, nnz), jnp.int32),
            pltpu.SMEM((nblk * nblk // nnz, nnz), jnp.int32),
            pltpu.VMEM((rows, width), jnp.float32),
            pltpu.VMEM((GROUPS, 2, per_dir, group, CHUNK), jnp.bfloat16),
            pltpu.VMEM((GROUPS, 2, per_dir, group, CHUNK), jnp.bfloat16),
            pltpu.SemaphoreType.DMA((4 + PARTS,)),
            pltpu.SemaphoreType.DMA((GROUPS, 2, per_dir)),
            pltpu.SemaphoreType.DMA((GROUPS, 2, per_dir)),
        ],
        compiler_params=pltpu.CompilerParams(collective_id=0, has_side_effects=True),
    )(
        blocks.reshape(nnz, order, order),
        pattern.reshape(1, nnz),
        local_src.reshape(rows, width),
        owner,
    )
    return result.reshape(1, 1, nbatch, nsource, width)


def solution(mesh):
    return jax.shard_map(
        functools.partial(body, mesh.shape["gx"], mesh.shape["gy"]),
        mesh=mesh,
        in_specs=(
            P("gx", "gy", None, None, None),
            P("gx", "gy", None),
            P("gx", "gy", None, None, None),
            P(),
        ),
        out_specs=P("gx", "gy", None, None, None),
        check_vma=False,
    )
```
